512 devices in a mesh: node: 128 (over z, x, core), hub: 4 (over y).
Axes of the slice: x: 4, y: 4, z: 16, core: 2. Of those that a mesh axis runs over, the one named last changes fastest.
Arguments:
- node_state: bfloat16 [32768, 256], P('node'), may hold values from -7 to 7
- w_source: bfloat16 [256, 256], replicated, may hold values from -0.375 to 0.375
- w_target: bfloat16 [256, 256], replicated, may hold values from -0.375 to 0.375
- type_table: bfloat16 [4, 256], replicated, may hold values from -5 to 5
- attention: float32 [8, 32], replicated, may hold values from -28 to 28
- w_input: bfloat16 [256, 768], replicated, may hold values from -0.375 to 0.375
- w_hidden: bfloat16 [256, 768], replicated, may hold values from -0.375 to 0.375
- edge_src: int32 [524288], P(('node', 'hub')), may hold values from 0 to 32767, as said below
- edge_dst: int32 [524288], P(('node', 'hub')), may hold values from 0 to 255, as said below
- edge_type: int32 [524288], P(('node', 'hub')), may hold values from 0 to 2, as said below
- edge_live: int32 [524288], P(('node', 'hub')), may hold values from 0 to 1, as said below
Outputs:
- new_state: bfloat16 [32768, 256], P('node')
The draws below stay inside these ranges and needn't reach their ends.
Inputs may be any that keep to these rules, and one draw needn't show every extreme that they name: `edge_src`: A device's 1024 slots form 128 blocks of 8; the sources of block k lie in node partition k (nodes k * 256 to (k + 1) * 256 - 1). The sources of one block, live or not, are at most 2 distinct nodes, and exactly 2 in every block. `edge_dst`: destination's index within the node partition of the device. `edge_type`: the last type is never on an edge slot. `edge_live`: within each block of 8 slots the live ones come first; each block has at least one live slot, and each device has a block with all 8 live.
All inputs are finite; a program needn't handle non-finite values.
Results may differ from the reference program's by a relative error of at most 0.012.
Values may be sent and summed in bfloat16 or wider, within the bound.
A program may use at most 64 MiB of HBM per device.

```python
import jax
import jax.numpy as jnp
from jax import lax

D = 256
HEADS = 8
HEAD_DIM = 32
TYPES = 4
NODE_DEV = 256
CAP = 8
UNIQ = 2
NODES = 32768
N_NODE = 128
N_HUB = 4


def edge_tables(key):
    base = jax.random.fold_in(key, 7)
    keys = jax.random.split(base, 9)
    blocks = (N_NODE, N_HUB, N_NODE)
    spacing = NODE_DEV // UNIQ
    offsets = jax.random.randint(keys[0], blocks + (UNIQ,), 0, spacing)
    candidates = jnp.arange(UNIQ, dtype=jnp.int32) * spacing + offsets
    slot = jnp.arange(CAP, dtype=jnp.int32)
    picks = jax.random.randint(keys[1], blocks + (CAP,), 0, UNIQ)
    picks = jnp.where(slot < UNIQ, slot, picks)
    chosen = jnp.take_along_axis(candidates, picks, axis=3)
    owner = jnp.arange(N_NODE, dtype=jnp.int32)[None, None, :, None]
    sources = owner * NODE_DEV + chosen
    counts = jax.random.randint(keys[2], blocks, 1, CAP + 1)
    full = jax.random.randint(keys[3], (N_NODE, N_HUB), 0, N_NODE)
    counts = jnp.where(jnp.arange(N_NODE, dtype=jnp.int32)[None, None, :] == full[:, :, None], CAP, counts)
    live = (slot[None, None, None, :] < counts[..., None]).astype(jnp.int32)
    hub_spacing = NODE_DEV // 4
    hubs = jnp.arange(4, dtype=jnp.int32) * hub_spacing + jax.random.randint(keys[4], (N_NODE, 4), 0, hub_spacing)
    which = jax.random.randint(keys[5], blocks + (CAP,), 0, 4)
    hub_dest = jnp.take_along_axis(jnp.broadcast_to(hubs[:, None, None, :], blocks + (4,)), which, axis=3)
    drawn = jax.random.randint(keys[6], blocks + (CAP,), 0, NODE_DEV)
    coin = jax.random.randint(keys[7], blocks + (CAP,), 0, 4)
    dests = jnp.where(coin == 0, hub_dest, drawn)
    kinds = jax.random.randint(keys[8], blocks + (CAP,), 0, TYPES - 1)
    return (sources.reshape(-1), dests.reshape(-1), kinds.reshape(-1), live.reshape(-1))


def draw_edge_src(key, part):
    return edge_tables(key)[0]


def draw_edge_dst(key, part):
    return edge_tables(key)[1]


def draw_edge_type(key, part):
    return edge_tables(key)[2]


def draw_edge_live(key, part):
    return edge_tables(key)[3]


def draw_node_state(key, part):
    first = jax.random.fold_in(jax.random.fold_in(key, 11), 0)
    values = jnp.clip(jax.random.normal(first, (NODES, D), jnp.float32), -4.0, 4.0)
    return values.astype(jnp.bfloat16)


def draw_attention(key, part):
    first = jax.random.fold_in(jax.random.fold_in(key, 13), 0)
    values = jnp.clip(jax.random.normal(first, (HEADS, HEAD_DIM), jnp.float32), -4.0, 4.0)
    return values


def centred(key, dims, scale, bound, kind=jnp.bfloat16):
    array = jax.random.normal(key, dims, jnp.float32) * scale
    return jnp.minimum(jnp.maximum(array, -bound), bound).astype(kind)


def setup_inputs(seed: int = 0) -> dict:
    arg_keys = jax.random.split(jax.random.key(seed), 12)
    return {
        "node_state": draw_node_state(jax.random.fold_in(arg_keys[11], 71), 0),
        "w_source": centred(arg_keys[1], (D, D), D ** -0.5, 0.375),
        "w_target": centred(arg_keys[2], (D, D), D ** -0.5, 0.375),
        "type_table": centred(arg_keys[3], (TYPES, D), 1.0, 5.0),
        "attention": draw_attention(jax.random.fold_in(arg_keys[11], 71), 0),
        "w_input": centred(arg_keys[5], (D, 3 * D), D ** -0.5, 0.375),
        "w_hidden": centred(arg_keys[6], (D, 3 * D), D ** -0.5, 0.375),
        "edge_src": draw_edge_src(jax.random.fold_in(arg_keys[11], 71), 0),
        "edge_dst": draw_edge_dst(jax.random.fold_in(arg_keys[11], 71), 0),
        "edge_type": draw_edge_type(jax.random.fold_in(arg_keys[11], 71), 0),
        "edge_live": draw_edge_live(jax.random.fold_in(arg_keys[11], 71), 0),
    }


big_value = 1e30


def attend(pre, attention):
    leaky = jnp.maximum(pre, 0.2 * pre)
    shaped = leaky.reshape(pre.shape[0], attention.shape[0], attention.shape[1])
    return jnp.sum(shaped * attention.astype(jnp.float32)[None, :, :], axis=2)


def spread(per_head, head_dim):
    return jnp.repeat(per_head, head_dim, axis=1)


def recurrent(agg, state, w_input, w_hidden):
    width = state.shape[1]
    from_input = jnp.dot(agg, w_input, preferred_element_type=jnp.float32)
    from_state = jnp.dot(state, w_hidden, preferred_element_type=jnp.float32)
    reset = jax.nn.sigmoid(from_input[:, :width] + from_state[:, :width])
    update = jax.nn.sigmoid(from_input[:, width:2 * width] + from_state[:, width:2 * width])
    candidate = jnp.tanh(from_input[:, 2 * width:] + reset * from_state[:, 2 * width:])
    return ((1.0 - update) * candidate + update * state.astype(jnp.float32)).astype(jnp.bfloat16)


def reference(node_state, w_source, w_target, type_table, attention, w_input, w_hidden, edge_src, edge_dst, edge_type, edge_live):
    width = node_state.shape[1]
    source = jnp.dot(node_state, w_source, preferred_element_type=jnp.float32).astype(jnp.bfloat16)
    target = jnp.dot(node_state, w_target, preferred_element_type=jnp.float32)
    kinds_table = type_table.astype(jnp.float32)

    def one_part(items):
        src, dst, kinds, live, own, tgt, state = items
        rows = source[src].astype(jnp.float32)
        own_rows = own.astype(jnp.float32)
        pre = rows + tgt[dst] + kinds_table[kinds]
        alive = live[:, None] > 0
        score = jnp.where(alive, attend(pre, attention), -big_value)
        self_score = attend(own_rows + tgt + kinds_table[TYPES - 1][None, :], attention)
        peak = jnp.maximum(jax.ops.segment_max(score, dst, num_segments=NODE_DEV), self_score)
        weight = jnp.where(alive, jnp.exp(score - peak[dst]), 0.0)
        self_weight = jnp.exp(self_score - peak)
        total = jax.ops.segment_sum(weight, dst, num_segments=NODE_DEV) + self_weight
        value = jax.ops.segment_sum(spread(weight, HEAD_DIM) * rows, dst, num_segments=NODE_DEV)
        value = value + spread(self_weight, HEAD_DIM) * own_rows
        agg = (value / spread(total, HEAD_DIM)).astype(jnp.bfloat16)
        return recurrent(agg, state, w_input, w_hidden)

    items = (edge_src.reshape(N_NODE, -1), edge_dst.reshape(N_NODE, -1), edge_type.reshape(N_NODE, -1),
             edge_live.reshape(N_NODE, -1), source.reshape(N_NODE, NODE_DEV, width),
             target.reshape(N_NODE, NODE_DEV, width), node_state.reshape(N_NODE, NODE_DEV, width))
    return lax.map(one_part, items).reshape(NODES, width)
```

```python
import functools

import jax
import jax.numpy as jnp
from jax import lax
from jax.experimental import pallas as pl
from jax.experimental.pallas import tpu as pltpu
from jax.sharding import PartitionSpec as P

f32 = jnp.float32
bf16 = jnp.bfloat16
big_value = 1e30
MESH = pl.DeviceIdType.MESH
GROUP = 128


def halves(x):
    high = x.astype(bf16)
    return high, (x - high.astype(f32)).astype(bf16)


def dot(a, b):
    return jnp.dot(a, b, preferred_element_type=f32)


def dot_nt(a, b):
    return lax.dot_general(a, b, (((1,), (1,)), ((), ())), preferred_element_type=f32)


def leaky(v):
    return jnp.maximum(v, 0.2 * v)


def lane_ids(rows, lanes):
    return lax.broadcasted_iota(jnp.int32, (rows, lanes), 1).astype(f32)


def columns(flat):
    return jnp.transpose(flat.astype(f32))


def requests(src_cols, slots, node_dev):
    lanes, groups = src_cols.shape
    per = lanes // slots
    cube = src_cols.reshape(per, slots, groups)
    low = jnp.min(cube, axis=1)
    high = jnp.max(cube, axis=1)
    picked = jnp.where(cube == jnp.max(cube, axis=1, keepdims=True), 1.0, 0.0).reshape(lanes, groups)
    lane = lax.broadcasted_iota(jnp.int32, (per, 128), 1)
    row = lax.broadcasted_iota(jnp.int32, (per, 128), 0)
    out = []
    for g in range(groups):
        first = ((g * per + row) * node_dev).astype(f32)
        out.append(jnp.where(lane == 0, low[:, g : g + 1], high[:, g : g + 1]) - first)
    return out, picked


def owner_rows(asked, source):
    peers, node_dev = asked.shape[0], source.shape[0]
    ids = lane_ids(peers, node_dev)
    first = dot(jnp.where(ids == asked[:, 0:1], 1.0, 0.0).astype(bf16), source)
    second = dot(jnp.where(ids == asked[:, 1:2], 1.0, 0.0).astype(bf16), source)
    return jnp.stack([first, second], axis=1).astype(bf16)


def head_matrix(attention, width):
    heads, head_dim = attention.shape
    wide = jnp.concatenate([attention] * heads, axis=1)
    return jnp.where(head_mask(heads, width), wide, 0.0)


def head_mask(heads, width):
    head_dim = width // heads
    lane = lax.broadcasted_iota(jnp.int32, (heads, width), 1)
    row = lax.broadcasted_iota(jnp.int32, (heads, width), 0)
    return (lane >= row * head_dim) & (lane < (row + 1) * head_dim)


def scores(left, att_high, att_low):
    high, low = halves(left)
    return dot_nt(high, att_high) + (dot_nt(high, att_low) + dot_nt(low, att_high))


def scores_t(left, att_high, att_low):
    high, low = halves(left)
    return dot_nt(att_high, high) + (dot_nt(att_low, high) + dot_nt(att_high, low))


def merge(peaks, totals, values, self_t, source, expand):
    peak = self_t
    for p in peaks:
        peak = jnp.maximum(peak, p)
    scales = [jnp.exp(p - peak) for p in peaks]
    self_scale = jnp.exp(self_t - peak)
    total = self_scale
    for s, t in zip(scales, totals):
        total = total + s * t
    inverse = 1.0 / total
    coefs = jnp.concatenate([s * inverse for s in scales] + [self_scale * inverse], axis=0)
    high, low = halves(jnp.transpose(coefs))
    heads = self_t.shape[0]
    agg = None
    for d, value in enumerate(list(values) + [source]):
        part = slice(d * heads, (d + 1) * heads)
        factor = dot(high[:, part], expand) + dot(low[:, part], expand)
        term = factor * value.astype(f32)
        agg = term if agg is None else agg + term
    return agg.astype(bf16)


def gru(agg, from_state, state, w_input):
    width = state.shape[1]
    from_input = dot(agg, w_input)
    reset = jax.nn.sigmoid(from_input[:, :width] + from_state[:, :width])
    update = jax.nn.sigmoid(from_input[:, width : 2 * width] + from_state[:, width : 2 * width])
    candidate = jnp.tanh(from_input[:, 2 * width :] + reset * from_state[:, 2 * width :])
    return ((1.0 - update) * candidate + update * state.astype(f32)).astype(bf16)


def kernel(
    peers,
    hubs,
    state_ref,
    w_source_ref,
    w_target_ref,
    type_ref,
    attention_ref,
    w_input_ref,
    w_hidden_ref,
    src_ref,
    dst_ref,
    kind_ref,
    live_ref,
    out_ref,
    ask_out,
    ask_in,
    row_out,
    row_in,
    source_ref,
    member_ref,
    member_t_ref,
    pick_ref,
    base_ref,
    mask_ref,
    dead_ref,
    score_ref,
    rows_ref,
    value_ref,
    stat_ref,
    value_in,
    stat_in,
    from_state_ref,
    ask_send,
    ask_recv,
    ask_own,
    row_send,
    row_recv,
    row_own,
    value_send,
    value_recv,
    stat_send,
    stat_recv,
):
    me = lax.axis_index("node")
    hub = lax.axis_index("hub")
    node_dev, width = state_ref.shape
    heads = attention_ref.shape[0]
    groups = src_ref.shape[0]
    slots = groups * 128 // peers

    def each_peer(act):
        act(lax.rem(me + peers // 2, peers))

        def step(t, carry):
            act(lax.rem(me + (peers // 2 + 1 + t), peers))
            act(lax.rem(me + (peers // 2 - 1 - t), peers))
            return carry

        lax.fori_loop(0, peers // 2 - 1, step, 0)

    barrier = pltpu.get_barrier_semaphore()

    def greet(peer):
        pl.semaphore_signal(barrier, inc=1, device_id=(peer, hub), device_id_type=MESH)

    each_peer(greet)
    for h in range(1, hubs):
        pl.semaphore_signal(
            barrier, inc=1, device_id=(me, lax.rem(hub + h, hubs)), device_id_type=MESH
        )

    asks, picked = requests(columns(src_ref[...]), slots, node_dev)
    per = peers // groups
    for g in range(groups):
        ask_out[g * per : (g + 1) * per, 0, :] = asks[g]
    state = state_ref[...]
    source = dot(state, w_source_ref[...]).astype(bf16)
    source_ref[...] = source

    pl.semaphore_wait(barrier, peers - 1 + hubs - 1)

    def ask(peer):
        pltpu.make_async_remote_copy(
            src_ref=ask_out.at[peer],
            dst_ref=ask_in.at[me],
            send_sem=ask_send,
            recv_sem=ask_recv,
            device_id=(peer, hub),
            device_id_type=MESH,
        ).start()

    each_peer(ask)
    own_ask = pltpu.make_async_copy(ask_out.at[me], ask_in.at[me], ask_own)
    own_ask.start()

    target = dot(state, w_target_ref[...])
    target_high, target_low = halves(target)
    types = type_ref[...].astype(f32)
    att = head_matrix(attention_ref[...], width)
    att_high, att_low = halves(att)
    expand = jnp.where(head_mask(heads, width), 1.0, 0.0).astype(bf16)
    self_t = scores_t(
        leaky(source.astype(f32) + target + types[types.shape[0] - 1 :, :]), att_high, att_low
    )
    dst_cols = columns(dst_ref[...])
    kind_cols = columns(kind_ref[...])
    live_cols = columns(live_ref[...])
    ids = lane_ids(GROUP, node_dev)
    block = (lax.broadcasted_iota(jnp.int32, (GROUP, 1), 0) // slots).astype(f32)
    node_ids = lax.broadcasted_iota(jnp.int32, (node_dev, GROUP), 0)
    for g in range(groups):
        part = slice(g * GROUP, (g + 1) * GROUP)
        here = ids == dst_cols[:, g : g + 1]
        member = jnp.where(here, 1.0, 0.0).astype(bf16)
        member_ref[part, :] = member
        mask_ref[part, :] = jnp.where(here, 0.0, -big_value)
        member_t_ref[:, part] = jnp.where(node_ids == dst_ref[g : g + 1, :], 1.0, 0.0).astype(bf16)
        wanted = 2.0 * (g * (GROUP // slots) + block) + picked[:, g : g + 1]
        pick_ref[part, :] = jnp.where(lane_ids(GROUP, 2 * peers) == wanted, 1.0, 0.0).astype(bf16)
        kind = kind_cols[:, g : g + 1]
        kinds = types[0:1, :]
        for t in range(1, types.shape[0]):
            kinds = jnp.where(kind == float(t), types[t : t + 1, :], kinds)
        base_ref[part, :] = dot(member, target_high) + dot(member, target_low) + kinds
        dead_ref[part, :] = jnp.broadcast_to(
            jnp.where(live_cols[:, g : g + 1] > 0.0, 0.0, -big_value), (GROUP, heads)
        )

    own_ask.wait()
    pltpu.make_async_copy(
        ask_in.at[pl.ds(0, peers - 1)], ask_in.at[pl.ds(0, peers - 1)], ask_recv
    ).wait()
    row_out[...] = owner_rows(ask_in[:, 0, :], source_ref[...])

    def reply(peer):
        pltpu.make_async_remote_copy(
            src_ref=row_out.at[peer],
            dst_ref=row_in.at[me],
            send_sem=row_send,
            recv_sem=row_recv,
            device_id=(peer, hub),
            device_id_type=MESH,
        ).start()

    each_peer(reply)
    own_row = pltpu.make_async_copy(row_out.at[me], row_in.at[me], row_own)
    own_row.start()
    from_state_ref[...] = dot(state_ref[...], w_hidden_ref[...])
    pltpu.make_async_copy(
        ask_out.at[pl.ds(0, peers - 1)], ask_out.at[pl.ds(0, peers - 1)], ask_send
    ).wait()
    own_row.wait()
    pltpu.make_async_copy(
        row_in.at[pl.ds(0, peers - 1)], row_in.at[pl.ds(0, peers - 1)], row_recv
    ).wait()

    fetched = row_in[...].reshape(2 * peers, width)

    def score_step(g, peaks):
        part = pl.ds(pl.multiple_of(g * GROUP, GROUP), GROUP)
        rows = dot(pick_ref[part, :], fetched)
        rows_ref[part, :] = rows.astype(bf16)
        score = scores(leaky(rows + base_ref[part, :]), att_high, att_low) + dead_ref[part, :]
        score_ref[part, :] = score
        mask = mask_ref[part, :]
        fresh = [jnp.max(score[:, h : h + 1] + mask, axis=0, keepdims=True) for h in range(heads)]
        return jnp.maximum(peaks, jnp.concatenate(fresh, axis=0))

    peak = lax.fori_loop(0, groups, score_step, self_t)
    peak_high, peak_low = halves(peak)
    peak = peak_high.astype(f32) + peak_low.astype(f32)

    def weigh_step(g, carry):
        value, total = carry
        part = pl.ds(pl.multiple_of(g * GROUP, GROUP), GROUP)
        member = member_ref[part, :]
        edge_peak = dot_nt(member, peak_high) + dot_nt(member, peak_low)
        weight = jnp.exp(score_ref[part, :] - edge_peak).astype(bf16)
        weighted = (dot(weight, expand) * rows_ref[part, :].astype(f32)).astype(bf16)
        member_t = member_t_ref[:, part]
        return value + dot(member_t, weighted), total + dot(member_t, weight)

    value, total = lax.fori_loop(
        0,
        groups,
        weigh_step,
        (jnp.zeros((node_dev, width), f32), jnp.zeros((node_dev, heads), f32)),
    )
    value_ref[...] = value.astype(bf16)
    stat_ref[0:heads, :] = peak
    stat_ref[heads : 2 * heads, :] = jnp.transpose(total)

    copies = []
    for h in range(1, hubs):
        other = (me, lax.rem(hub + h, hubs))
        for source_buf, target_buf, send, recv in (
            (stat_ref, stat_in, stat_send, stat_recv),
            (value_ref, value_in, value_send, value_recv),
        ):
            copy = pltpu.make_async_remote_copy(
                src_ref=source_buf,
                dst_ref=target_buf.at[h - 1],
                send_sem=send.at[h - 1],
                recv_sem=recv.at[h - 1],
                device_id=other,
                device_id_type=MESH,
            )
            copy.start()
            copies.append(copy)
    for copy in copies:
        copy.wait()
    pltpu.make_async_copy(
        row_out.at[pl.ds(0, peers - 1)], row_out.at[pl.ds(0, peers - 1)], row_send
    ).wait()

    stats = [stat_ref[...]] + [stat_in[h] for h in range(hubs - 1)]
    agg = merge(
        [s[0:heads, :] for s in stats],
        [s[heads : 2 * heads, :] for s in stats],
        [value_ref[...]] + [value_in[h] for h in range(hubs - 1)],
        self_t,
        source_ref[...],
        expand,
    )
    out_ref[...] = gru(agg, from_state_ref[...], state_ref[...], w_input_ref[...])


def body(
    node_state,
    w_source,
    w_target,
    type_table,
    attention,
    w_input,
    w_hidden,
    edge_src,
    edge_dst,
    edge_type,
    edge_live,
):
    peers = lax.axis_size("node")
    hubs = lax.axis_size("hub")
    node_dev, width = node_state.shape
    heads = attention.shape[0]
    edges = edge_src.shape[0]
    dma = pltpu.SemaphoreType.DMA
    vmem = pltpu.VMEM
    return pl.pallas_call(
        functools.partial(kernel, peers, hubs),
        out_shape=jax.ShapeDtypeStruct((node_dev, width), bf16),
        in_specs=[pl.BlockSpec(memory_space=pltpu.VMEM)] * 11,
        out_specs=pl.BlockSpec(memory_space=pltpu.VMEM),
        scratch_shapes=[
            vmem((peers, 1, 128), f32),
            vmem((peers, 1, 128), f32),
            vmem((peers, 2, width), bf16),
            vmem((peers, 2, width), bf16),
            vmem((node_dev, width), bf16),
            vmem((edges, node_dev), bf16),
            vmem((node_dev, edges), bf16),
            vmem((edges, 2 * peers), bf16),
            vmem((edges, width), f32),
            vmem((edges, node_dev), f32),
            vmem((edges, heads), f32),
            vmem((edges, heads), f32),
            vmem((edges, width), bf16),
            vmem((node_dev, width), bf16),
            vmem((2 * heads, node_dev), f32),
            vmem((hubs - 1, node_dev, width), bf16),
            vmem((hubs - 1, 2 * heads, node_dev), f32),
            vmem((node_dev, 3 * width), f32),
            dma,
            dma,
            dma,
            dma,
            dma,
            dma,
            dma((hubs - 1,)),
            dma((hubs - 1,)),
            dma((hubs - 1,)),
            dma((hubs - 1,)),
        ],
        compiler_params=pltpu.CompilerParams(collective_id=0, has_side_effects=True),
        name="gat",
    )(
        node_state,
        w_source,
        w_target,
        type_table,
        attention,
        w_input,
        w_hidden,
        edge_src.reshape(-1, 128),
        edge_dst.reshape(-1, 128),
        edge_type.reshape(-1, 128),
        edge_live.reshape(-1, 128),
    )


def solution(mesh):
    edges = P(("node", "hub"))
    placed = (P("node", None), P(), P(), P(), P(), P(), P(), edges, edges, edges, edges)
    return jax.shard_map(
        body, mesh=mesh, in_specs=placed, out_specs=P("node", None), check_vma=False
    )
```

```python
import functools

import jax
import jax.numpy as jnp
from jax import lax
from jax.experimental import pallas as pl
from jax.experimental.pallas import tpu as pltpu
from jax.sharding import PartitionSpec as P

f32 = jnp.float32
bf16 = jnp.bfloat16
big_value = 1e30
MESH = pl.DeviceIdType.MESH
GROUP = 128


def halves(x):
    high = x.astype(bf16)
    return high, (x - high.astype(f32)).astype(bf16)


def dot(a, b):
    return jnp.dot(a, b, preferred_element_type=f32)


def dot_nt(a, b):
    return lax.dot_general(a, b, (((1,), (1,)), ((), ())), preferred_element_type=f32)


def leaky(v):
    return jnp.maximum(v, 0.2 * v)


def lane_ids(rows, lanes):
    return lax.broadcasted_iota(jnp.int32, (rows, lanes), 1).astype(f32)


def columns(flat):
    return jnp.transpose(flat.astype(f32))


def requests(src_cols, slots, node_dev):
    lanes, groups = src_cols.shape
    per = lanes // slots
    cube = src_cols.reshape(per, slots, groups)
    low = jnp.min(cube, axis=1)
    high = jnp.max(cube, axis=1)
    picked = jnp.where(cube == jnp.max(cube, axis=1, keepdims=True), 1.0, 0.0).reshape(lanes, groups)
    lane = lax.broadcasted_iota(jnp.int32, (per, 128), 1)
    row = lax.broadcasted_iota(jnp.int32, (per, 128), 0)
    out = []
    for g in range(groups):
        first = ((g * per + row) * node_dev).astype(f32)
        out.append(jnp.where(lane == 0, low[:, g : g + 1], high[:, g : g + 1]) - first)
    return out, picked


def owner_rows(asked, source):
    peers, node_dev = asked.shape[0], source.shape[0]
    ids = lane_ids(peers, node_dev)
    first = dot(jnp.where(ids == asked[:, 0:1], 1.0, 0.0).astype(bf16), source)
    second = dot(jnp.where(ids == asked[:, 1:2], 1.0, 0.0).astype(bf16), source)
    return jnp.stack([first, second], axis=1).astype(bf16)


def head_matrix(attention, width):
    heads, head_dim = attention.shape
    wide = jnp.concatenate([attention] * heads, axis=1)
    return jnp.where(head_mask(heads, width), wide, 0.0)


def head_mask(heads, width):
    head_dim = width // heads
    lane = lax.broadcasted_iota(jnp.int32, (heads, width), 1)
    row = lax.broadcasted_iota(jnp.int32, (heads, width), 0)
    return (lane >= row * head_dim) & (lane < (row + 1) * head_dim)


def scores(left, att_high, att_low):
    high, low = halves(left)
    return dot_nt(high, att_high) + (dot_nt(high, att_low) + dot_nt(low, att_high))


def scores_t(left, att_high, att_low):
    high, low = halves(left)
    return dot_nt(att_high, high) + (dot_nt(att_low, high) + dot_nt(att_high, low))


def merge(peaks, totals, values, self_t, source, expand):
    peak = self_t
    for p in peaks:
        peak = jnp.maximum(peak, p)
    scales = [jnp.exp(p - peak) for p in peaks]
    self_scale = jnp.exp(self_t - peak)
    total = self_scale
    for s, t in zip(scales, totals):
        total = total + s * t
    inverse = 1.0 / total
    coefs = jnp.concatenate([s * inverse for s in scales] + [self_scale * inverse], axis=0)
    high, low = halves(jnp.transpose(coefs))
    heads = self_t.shape[0]
    agg = None
    for d, value in enumerate(list(values) + [source]):
        part = slice(d * heads, (d + 1) * heads)
        factor = dot(high[:, part], expand) + dot(low[:, part], expand)
        term = factor * value.astype(f32)
        agg = term if agg is None else agg + term
    return agg.astype(bf16)


def gru(agg, from_state, state, w_input):
    width = state.shape[1]
    from_input = dot(agg, w_input)
    reset = jax.nn.sigmoid(from_input[:, :width] + from_state[:, :width])
    update = jax.nn.sigmoid(from_input[:, width : 2 * width] + from_state[:, width : 2 * width])
    candidate = jnp.tanh(from_input[:, 2 * width :] + reset * from_state[:, 2 * width :])
    return ((1.0 - update) * candidate + update * state.astype(f32)).astype(bf16)


def kernel(
    peers,
    hubs,
    state_ref,
    w_source_ref,
    w_target_ref,
    type_ref,
    attention_ref,
    w_input_ref,
    w_hidden_ref,
    src_ref,
    dst_ref,
    kind_ref,
    live_ref,
    out_ref,
    ask_out,
    ask_in,
    row_out,
    row_in,
    source_ref,
    member_ref,
    member_t_ref,
    pick_ref,
    base_ref,
    mask_ref,
    dead_ref,
    score_ref,
    rows_ref,
    value_ref,
    stat_ref,
    value_in,
    stat_in,
    from_state_ref,
    self_ref,
    done_ref,
    ask_send,
    ask_recv,
    ask_own,
    row_send,
    row_recv,
    row_own,
    value_send,
    value_recv,
    stat_send,
    stat_recv,
    done_send,
    done_recv,
):
    me = lax.axis_index("node")
    hub = lax.axis_index("hub")
    node_dev, width = state_ref.shape
    heads = attention_ref.shape[0]
    groups = src_ref.shape[0]
    slots = groups * 128 // peers

    def each_peer(act):
        act(lax.rem(me + peers // 2, peers))

        def step(t, carry):
            act(lax.rem(me + (peers // 2 + 1 + t), peers))
            act(lax.rem(me + (peers // 2 - 1 - t), peers))
            return carry

        lax.fori_loop(0, peers // 2 - 1, step, 0)

    barrier = pltpu.get_barrier_semaphore()

    def greet(peer):
        pl.semaphore_signal(barrier, inc=1, device_id=(peer, hub), device_id_type=MESH)

    each_peer(greet)
    for h in range(1, hubs):
        pl.semaphore_signal(
            barrier, inc=1, device_id=(me, lax.rem(hub + h, hubs)), device_id_type=MESH
        )

    asks, picked = requests(columns(src_ref[...]), slots, node_dev)
    per = peers // groups
    for g in range(groups):
        ask_out[g * per : (g + 1) * per, 0, :] = asks[g]
    state = state_ref[...]
    source = dot(state, w_source_ref[...]).astype(bf16)
    source_ref[...] = source

    pl.semaphore_wait(barrier, peers - 1 + hubs - 1)

    def ask(peer):
        pltpu.make_async_remote_copy(
            src_ref=ask_out.at[peer],
            dst_ref=ask_in.at[me],
            send_sem=ask_send,
            recv_sem=ask_recv,
            device_id=(peer, hub),
            device_id_type=MESH,
        ).start()

    each_peer(ask)
    own_ask = pltpu.make_async_copy(ask_out.at[me], ask_in.at[me], ask_own)
    own_ask.start()

    target = dot(state, w_target_ref[...])
    target_high, target_low = halves(target)
    types = type_ref[...].astype(f32)
    att = head_matrix(attention_ref[...], width)
    att_high, att_low = halves(att)
    expand = jnp.where(head_mask(heads, width), 1.0, 0.0).astype(bf16)
    self_t = scores_t(
        leaky(source.astype(f32) + target + types[types.shape[0] - 1 :, :]), att_high, att_low
    )
    dst_cols = columns(dst_ref[...])
    kind_cols = columns(kind_ref[...])
    live_cols = columns(live_ref[...])
    ids = lane_ids(GROUP, node_dev)
    block = (lax.broadcasted_iota(jnp.int32, (GROUP, 1), 0) // slots).astype(f32)
    node_ids = lax.broadcasted_iota(jnp.int32, (node_dev, GROUP), 0)
    for g in range(groups):
        part = slice(g * GROUP, (g + 1) * GROUP)
        here = ids == dst_cols[:, g : g + 1]
        member = jnp.where(here, 1.0, 0.0).astype(bf16)
        member_ref[part, :] = member
        mask_ref[part, :] = jnp.where(here, 0.0, -big_value)
        member_t_ref[:, part] = jnp.where(node_ids == dst_ref[g : g + 1, :], 1.0, 0.0).astype(bf16)
        wanted = 2.0 * (g * (GROUP // slots) + block) + picked[:, g : g + 1]
        pick_ref[part, :] = jnp.where(lane_ids(GROUP, 2 * peers) == wanted, 1.0, 0.0).astype(bf16)
        kind = kind_cols[:, g : g + 1]
        kinds = types[0:1, :]
        for t in range(1, types.shape[0]):
            kinds = jnp.where(kind == float(t), types[t : t + 1, :], kinds)
        base_ref[part, :] = dot(member, target_high) + dot(member, target_low) + kinds
        dead_ref[part, :] = jnp.broadcast_to(
            jnp.where(live_cols[:, g : g + 1] > 0.0, 0.0, -big_value), (GROUP, heads)
        )

    own_ask.wait()
    pltpu.make_async_copy(
        ask_in.at[pl.ds(0, peers - 1)], ask_in.at[pl.ds(0, peers - 1)], ask_recv
    ).wait()
    row_out[...] = owner_rows(ask_in[:, 0, :], source_ref[...])

    def reply(peer):
        pltpu.make_async_remote_copy(
            src_ref=row_out.at[peer],
            dst_ref=row_in.at[me],
            send_sem=row_send,
            recv_sem=row_recv,
            device_id=(peer, hub),
            device_id_type=MESH,
        ).start()

    each_peer(reply)
    own_row = pltpu.make_async_copy(row_out.at[me], row_in.at[me], row_own)
    own_row.start()
    from_state_ref[...] = dot(state_ref[...], w_hidden_ref[...])
    pltpu.make_async_copy(
        ask_out.at[pl.ds(0, peers - 1)], ask_out.at[pl.ds(0, peers - 1)], ask_send
    ).wait()
    own_row.wait()
    pltpu.make_async_copy(
        row_in.at[pl.ds(0, peers - 1)], row_in.at[pl.ds(0, peers - 1)], row_recv
    ).wait()

    fetched = row_in[...].reshape(2 * peers, width)

    def score_step(g, peaks):
        part = pl.ds(pl.multiple_of(g * GROUP, GROUP), GROUP)
        rows = dot(pick_ref[part, :], fetched)
        rows_ref[part, :] = rows.astype(bf16)
        score = scores(leaky(rows + base_ref[part, :]), att_high, att_low) + dead_ref[part, :]
        score_ref[part, :] = score
        mask = mask_ref[part, :]
        fresh = [jnp.max(score[:, h : h + 1] + mask, axis=0, keepdims=True) for h in range(heads)]
        return jnp.maximum(peaks, jnp.concatenate(fresh, axis=0))

    peak = lax.fori_loop(0, groups, score_step, self_t)
    peak_high, peak_low = halves(peak)
    peak = peak_high.astype(f32) + peak_low.astype(f32)

    def weigh_step(g, carry):
        value, total = carry
        part = pl.ds(pl.multiple_of(g * GROUP, GROUP), GROUP)
        member = member_ref[part, :]
        edge_peak = dot_nt(member, peak_high) + dot_nt(member, peak_low)
        weight = jnp.exp(score_ref[part, :] - edge_peak).astype(bf16)
        weighted = (dot(weight, expand) * rows_ref[part, :].astype(f32)).astype(bf16)
        member_t = member_t_ref[:, part]
        return value + dot(member_t, weighted), total + dot(member_t, weight)

    value, total = lax.fori_loop(
        0,
        groups,
        weigh_step,
        (jnp.zeros((node_dev, width), f32), jnp.zeros((node_dev, heads), f32)),
    )
    value_ref[...] = value.astype(bf16)
    quarter = node_dev // hubs
    total_t = jnp.transpose(total)
    for h in range(hubs):
        nodes = slice(h * quarter, (h + 1) * quarter)
        stat_ref[h, 0:heads, 0:quarter] = peak[:, nodes]
        stat_ref[h, heads : 2 * heads, 0:quarter] = total_t[:, nodes]
        self_ref[h, :, 0:quarter] = self_t[:, nodes]

    copies = []
    for h in range(1, hubs):
        other = lax.rem(hub + h, hubs)
        theirs = pl.ds(pl.multiple_of(other * quarter, quarter), quarter)
        for source_buf, target_buf, send, recv in (
            (stat_ref.at[other], stat_in, stat_send, stat_recv),
            (value_ref.at[theirs, :], value_in, value_send, value_recv),
        ):
            copy = pltpu.make_async_remote_copy(
                src_ref=source_buf,
                dst_ref=target_buf.at[h - 1],
                send_sem=send.at[h - 1],
                recv_sem=recv.at[h - 1],
                device_id=(me, other),
                device_id_type=MESH,
            )
            copy.start()
            copies.append(copy)
    pltpu.make_async_copy(
        row_out.at[pl.ds(0, peers - 1)], row_out.at[pl.ds(0, peers - 1)], row_send
    ).wait()
    mine = pl.ds(pl.multiple_of(hub * quarter, quarter), quarter)
    own_stat = stat_ref[hub][:, 0:quarter]
    own_self = self_ref[hub][:, 0:quarter]
    own_value = value_ref[mine, :]
    for copy in copies:
        copy.wait()

    stats = [own_stat] + [stat_in[h][:, 0:quarter] for h in range(hubs - 1)]
    agg = merge(
        [s[0:heads, :] for s in stats],
        [s[heads : 2 * heads, :] for s in stats],
        [own_value] + [value_in[h] for h in range(hubs - 1)],
        own_self,
        source_ref[mine, :],
        expand,
    )
    done_ref[...] = gru(agg, from_state_ref[mine, :], state_ref[mine, :], w_input_ref[...])
    copies = []
    for h in range(1, hubs):
        copy = pltpu.make_async_remote_copy(
            src_ref=done_ref,
            dst_ref=out_ref.at[mine, :],
            send_sem=done_send.at[h - 1],
            recv_sem=done_recv.at[h - 1],
            device_id=(me, lax.rem(hub + h, hubs)),
            device_id_type=MESH,
        )
        copy.start()
        copies.append(copy)
    out_ref[mine, :] = done_ref[...]
    for copy in copies:
        copy.wait()


def body(
    node_state,
    w_source,
    w_target,
    type_table,
    attention,
    w_input,
    w_hidden,
    edge_src,
    edge_dst,
    edge_type,
    edge_live,
):
    peers = lax.axis_size("node")
    hubs = lax.axis_size("hub")
    node_dev, width = node_state.shape
    heads = attention.shape[0]
    edges = edge_src.shape[0]
    quarter = node_dev // hubs
    dma = pltpu.SemaphoreType.DMA
    vmem = pltpu.VMEM
    return pl.pallas_call(
        functools.partial(kernel, peers, hubs),
        out_shape=jax.ShapeDtypeStruct((node_dev, width), bf16),
        in_specs=[pl.BlockSpec(memory_space=pltpu.VMEM)] * 11,
        out_specs=pl.BlockSpec(memory_space=pltpu.VMEM),
        scratch_shapes=[
            vmem((peers, 1, 128), f32),
            vmem((peers, 1, 128), f32),
            vmem((peers, 2, width), bf16),
            vmem((peers, 2, width), bf16),
            vmem((node_dev, width), bf16),
            vmem((edges, node_dev), bf16),
            vmem((node_dev, edges), bf16),
            vmem((edges, 2 * peers), bf16),
            vmem((edges, width), f32),
            vmem((edges, node_dev), f32),
            vmem((edges, heads), f32),
            vmem((edges, heads), f32),
            vmem((edges, width), bf16),
            vmem((node_dev, width), bf16),
            vmem((hubs, 2 * heads, 128), f32),
            vmem((hubs - 1, quarter, width), bf16),
            vmem((hubs - 1, 2 * heads, 128), f32),
            vmem((node_dev, 3 * width), f32),
            vmem((hubs, heads, 128), f32),
            vmem((quarter, width), bf16),
            dma,
            dma,
            dma,
            dma,
            dma,
            dma,
            dma((hubs - 1,)),
            dma((hubs - 1,)),
            dma((hubs - 1,)),
            dma((hubs - 1,)),
            dma((hubs - 1,)),
            dma((hubs - 1,)),
        ],
        compiler_params=pltpu.CompilerParams(collective_id=0, has_side_effects=True),
        name="gat",
    )(
        node_state,
        w_source,
        w_target,
        type_table,
        attention,
        w_input,
        w_hidden,
        edge_src.reshape(-1, 128),
        edge_dst.reshape(-1, 128),
        edge_type.reshape(-1, 128),
        edge_live.reshape(-1, 128),
    )


def solution(mesh):
    edges = P(("node", "hub"))
    placed = (P("node", None), P(), P(), P(), P(), P(), P(), edges, edges, edges, edges)
    return jax.shard_map(
        body, mesh=mesh, in_specs=placed, out_specs=P("node", None), check_vma=False
    )
```

```python
import functools

import jax
import jax.numpy as jnp
from jax import lax
from jax.experimental import pallas as pl
from jax.experimental.pallas import tpu as pltpu
from jax.sharding import PartitionSpec as P

f32 = jnp.float32
bf16 = jnp.bfloat16
big_value = 1e30
MESH = pl.DeviceIdType.MESH
GROUP = 128


def halves(x):
    high = x.astype(bf16)
    return high, (x - high.astype(f32)).astype(bf16)


def dot(a, b):
    return jnp.dot(a, b, preferred_element_type=f32)


def dot_nt(a, b):
    return lax.dot_general(a, b, (((1,), (1,)), ((), ())), preferred_element_type=f32)


def leaky(v):
    return jnp.maximum(v, 0.2 * v)


def lane_ids(rows, lanes):
    return lax.broadcasted_iota(jnp.int32, (rows, lanes), 1).astype(f32)


def columns(flat):
    return jnp.transpose(flat.astype(f32))


def requests(src_cols, slots, node_dev):
    lanes, groups = src_cols.shape
    per = lanes // slots
    cube = src_cols.reshape(per, slots, groups)
    low = jnp.min(cube, axis=1)
    high = jnp.max(cube, axis=1)
    picked = jnp.where(cube == jnp.max(cube, axis=1, keepdims=True), 1.0, 0.0).reshape(lanes, groups)
    lane = lax.broadcasted_iota(jnp.int32, (per, 128), 1)
    row = lax.broadcasted_iota(jnp.int32, (per, 128), 0)
    out = []
    for g in range(groups):
        first = ((g * per + row) * node_dev).astype(f32)
        out.append(jnp.where(lane == 0, low[:, g : g + 1], high[:, g : g + 1]) - first)
    return out, picked


def owner_rows(asked, source):
    peers, node_dev = asked.shape[0], source.shape[0]
    ids = lane_ids(peers, node_dev)
    first = dot(jnp.where(ids == asked[:, 0:1], 1.0, 0.0).astype(bf16), source)
    second = dot(jnp.where(ids == asked[:, 1:2], 1.0, 0.0).astype(bf16), source)
    return jnp.stack([first, second], axis=1).astype(bf16)


def head_matrix(attention, width):
    heads, head_dim = attention.shape
    wide = jnp.concatenate([attention] * heads, axis=1)
    return jnp.where(head_mask(heads, width), wide, 0.0)


def head_mask(heads, width):
    head_dim = width // heads
    lane = lax.broadcasted_iota(jnp.int32, (heads, width), 1)
    row = lax.broadcasted_iota(jnp.int32, (heads, width), 0)
    return (lane >= row * head_dim) & (lane < (row + 1) * head_dim)


def scores(left, att_high, att_low):
    high, low = halves(left)
    return dot_nt(high, att_high) + (dot_nt(high, att_low) + dot_nt(low, att_high))


def scores_t(left, att_high, att_low):
    high, low = halves(left)
    return dot_nt(att_high, high) + (dot_nt(att_low, high) + dot_nt(att_high, low))


def merge(peaks, totals, values, self_t, source, expand):
    peak = self_t
    for p in peaks:
        peak = jnp.maximum(peak, p)
    scales = [jnp.exp(p - peak) for p in peaks]
    self_scale = jnp.exp(self_t - peak)
    total = self_scale
    for s, t in zip(scales, totals):
        total = total + s * t
    inverse = 1.0 / total
    coefs = jnp.concatenate([s * inverse for s in scales] + [self_scale * inverse], axis=0)
    high, low = halves(jnp.transpose(coefs))
    heads = self_t.shape[0]
    agg = None
    for d, value in enumerate(list(values) + [source]):
        part = slice(d * heads, (d + 1) * heads)
        factor = dot(high[:, part], expand) + dot(low[:, part], expand)
        term = factor * value.astype(f32)
        agg = term if agg is None else agg + term
    return agg.astype(bf16)


def gru(agg, from_state, state, w_input):
    width = state.shape[1]
    from_input = dot(agg, w_input)
    reset = jax.nn.sigmoid(from_input[:, :width] + from_state[:, :width])
    update = jax.nn.sigmoid(from_input[:, width : 2 * width] + from_state[:, width : 2 * width])
    candidate = jnp.tanh(from_input[:, 2 * width :] + reset * from_state[:, 2 * width :])
    return ((1.0 - update) * candidate + update * state.astype(f32)).astype(bf16)


def kernel(
    peers,
    hubs,
    state_any,
    w_source_any,
    w_target_any,
    type_any,
    attention_any,
    w_input_any,
    w_hidden_any,
    src_any,
    dst_any,
    kind_any,
    live_any,
    out_ref,
    ask_out,
    ask_in,
    row_out,
    row_in,
    source_ref,
    member_ref,
    member_t_ref,
    pick_ref,
    base_ref,
    mask_ref,
    dead_ref,
    score_ref,
    rows_ref,
    value_ref,
    stat_ref,
    value_in,
    stat_in,
    from_state_ref,
    self_ref,
    done_ref,
    weighted_ref,
    weight_ref,
    ask_send,
    ask_recv,
    ask_own,
    row_send,
    row_recv,
    row_own,
    value_send,
    value_recv,
    stat_send,
    stat_recv,
    done_send,
    done_recv,
    load_sem,
    state_ref,
    w_source_ref,
    w_target_ref,
    type_ref,
    attention_ref,
    w_input_ref,
    w_hidden_ref,
    src_ref,
    dst_ref,
    kind_ref,
    live_ref,
):
    me = lax.axis_index("node")
    hub = lax.axis_index("hub")
    loads = {}
    for i, (name, far, near) in enumerate(
        (
            ("state", state_any, state_ref),
            ("w_source", w_source_any, w_source_ref),
            ("w_target", w_target_any, w_target_ref),
            ("type", type_any, type_ref),
            ("attention", attention_any, attention_ref),
            ("w_input", w_input_any, w_input_ref),
            ("w_hidden", w_hidden_any, w_hidden_ref),
            ("src", src_any, src_ref),
            ("dst", dst_any, dst_ref),
            ("kind", kind_any, kind_ref),
            ("live", live_any, live_ref),
        )
    ):
        loads[name] = pltpu.make_async_copy(far, near, load_sem.at[i])
    node_dev, width = state_ref.shape
    heads = attention_ref.shape[0]
    groups = src_ref.shape[0]
    slots = groups * 128 // peers

    def each_peer(act):
        act(lax.rem(me + peers // 2, peers))

        def step(t, carry):
            act(lax.rem(me + (peers // 2 + 1 + t), peers))
            act(lax.rem(me + (peers // 2 - 1 - t), peers))
            return carry

        lax.fori_loop(0, peers // 2 - 1, step, 0)

    barrier = pltpu.get_barrier_semaphore()

    def greet(peer):
        pl.semaphore_signal(barrier, inc=1, device_id=(peer, hub), device_id_type=MESH)

    each_peer(greet)
    for h in range(1, hubs):
        pl.semaphore_signal(
            barrier, inc=1, device_id=(me, lax.rem(hub + h, hubs)), device_id_type=MESH
        )

    for name in ("src", "state", "w_source"):
        loads[name].start()
    for name in loads:
        if name not in ("src", "state", "w_source"):
            loads[name].start()
    for name in ("src", "state", "w_source"):
        loads[name].wait()
    asks, picked = requests(columns(src_ref[...]), slots, node_dev)
    per = peers // groups
    for g in range(groups):
        ask_out[g * per : (g + 1) * per, 0, :] = asks[g]
    state = state_ref[...]
    source = dot(state, w_source_ref[...]).astype(bf16)
    source_ref[...] = source

    pl.semaphore_wait(barrier, peers - 1 + hubs - 1)

    def ask(peer):
        pltpu.make_async_remote_copy(
            src_ref=ask_out.at[peer],
            dst_ref=ask_in.at[me],
            send_sem=ask_send,
            recv_sem=ask_recv,
            device_id=(peer, hub),
            device_id_type=MESH,
        ).start()

    each_peer(ask)
    own_ask = pltpu.make_async_copy(ask_out.at[me], ask_in.at[me], ask_own)
    own_ask.start()

    for name in loads:
        if name not in ("src", "state", "w_source"):
            loads[name].wait()
    target = dot(state, w_target_ref[...])
    target_high, target_low = halves(target)
    types = type_ref[...].astype(f32)
    att = head_matrix(attention_ref[...], width)
    att_high, att_low = halves(att)
    expand = jnp.where(head_mask(heads, width), 1.0, 0.0).astype(bf16)
    self_t = scores_t(
        leaky(source.astype(f32) + target + types[types.shape[0] - 1 :, :]), att_high, att_low
    )
    dst_cols = columns(dst_ref[...])
    kind_cols = columns(kind_ref[...])
    live_cols = columns(live_ref[...])
    ids = lane_ids(GROUP, node_dev)
    block = (lax.broadcasted_iota(jnp.int32, (GROUP, 1), 0) // slots).astype(f32)
    node_ids = lax.broadcasted_iota(jnp.int32, (node_dev, GROUP), 0)
    for g in range(groups):
        part = slice(g * GROUP, (g + 1) * GROUP)
        here = ids == dst_cols[:, g : g + 1]
        member = jnp.where(here, 1.0, 0.0).astype(bf16)
        member_ref[part, :] = member
        mask_ref[part, :] = jnp.where(here, 0.0, -big_value)
        member_t_ref[:, part] = jnp.where(node_ids == dst_ref[g : g + 1, :], 1.0, 0.0).astype(bf16)
        wanted = 2.0 * (g * (GROUP // slots) + block) + picked[:, g : g + 1]
        pick_ref[part, :] = jnp.where(lane_ids(GROUP, 2 * peers) == wanted, 1.0, 0.0).astype(bf16)
        kind = kind_cols[:, g : g + 1]
        kinds = types[0:1, :]
        for t in range(1, types.shape[0]):
            kinds = jnp.where(kind == float(t), types[t : t + 1, :], kinds)
        base_ref[part, :] = dot(member, target_high) + dot(member, target_low) + kinds
        dead_ref[part, :] = jnp.broadcast_to(
            jnp.where(live_cols[:, g : g + 1] > 0.0, 0.0, -big_value), (GROUP, heads)
        )

    own_ask.wait()
    pltpu.make_async_copy(
        ask_in.at[pl.ds(0, peers - 1)], ask_in.at[pl.ds(0, peers - 1)], ask_recv
    ).wait()
    row_out[...] = owner_rows(ask_in[:, 0, :], source_ref[...])

    def reply(peer):
        pltpu.make_async_remote_copy(
            src_ref=row_out.at[peer],
            dst_ref=row_in.at[me],
            send_sem=row_send,
            recv_sem=row_recv,
            device_id=(peer, hub),
            device_id_type=MESH,
        ).start()

    each_peer(reply)
    own_row = pltpu.make_async_copy(row_out.at[me], row_in.at[me], row_own)
    own_row.start()
    from_state_ref[...] = dot(state_ref[...], w_hidden_ref[...])
    pltpu.make_async_copy(
        ask_out.at[pl.ds(0, peers - 1)], ask_out.at[pl.ds(0, peers - 1)], ask_send
    ).wait()
    own_row.wait()
    pltpu.make_async_copy(
        row_in.at[pl.ds(0, peers - 1)], row_in.at[pl.ds(0, peers - 1)], row_recv
    ).wait()

    fetched = row_in[...].reshape(2 * peers, width)

    peak = self_t
    for g in range(groups):
        part = slice(g * GROUP, (g + 1) * GROUP)
        rows = dot(pick_ref[part, :], fetched)
        rows_ref[part, :] = rows.astype(bf16)
        score = scores(leaky(rows + base_ref[part, :]), att_high, att_low) + dead_ref[part, :]
        score_ref[part, :] = score
        mask = mask_ref[part, :]
        fresh = [jnp.max(score[:, h : h + 1] + mask, axis=0, keepdims=True) for h in range(heads)]
        peak = jnp.maximum(peak, jnp.concatenate(fresh, axis=0))
    peak_high, peak_low = halves(peak)
    peak = peak_high.astype(f32) + peak_low.astype(f32)

    for g in range(groups):
        part = slice(g * GROUP, (g + 1) * GROUP)
        member = member_ref[part, :]
        edge_peak = dot_nt(member, peak_high) + dot_nt(member, peak_low)
        weight = jnp.exp(score_ref[part, :] - edge_peak).astype(bf16)
        weight_ref[part, :] = weight
        rows = rows_ref[part, :].astype(f32)
        weighted_ref[part, :] = (dot(weight, expand) * rows).astype(bf16)
    total = dot(member_t_ref[...], weight_ref[...])
    value = dot(member_t_ref[...], weighted_ref[...])
    value_ref[...] = value.astype(bf16)
    quarter = node_dev // hubs
    total_t = jnp.transpose(total)
    for h in range(hubs):
        nodes = slice(h * quarter, (h + 1) * quarter)
        stat_ref[h, 0:heads, 0:quarter] = peak[:, nodes]
        stat_ref[h, heads : 2 * heads, 0:quarter] = total_t[:, nodes]
        self_ref[h, :, 0:quarter] = self_t[:, nodes]

    copies = []
    for h in range(1, hubs):
        other = lax.rem(hub + h, hubs)
        theirs = pl.ds(pl.multiple_of(other * quarter, quarter), quarter)
        for source_buf, target_buf, send, recv in (
            (stat_ref.at[other], stat_in, stat_send, stat_recv),
            (value_ref.at[theirs, :], value_in, value_send, value_recv),
        ):
            copy = pltpu.make_async_remote_copy(
                src_ref=source_buf,
                dst_ref=target_buf.at[h - 1],
                send_sem=send.at[h - 1],
                recv_sem=recv.at[h - 1],
                device_id=(me, other),
                device_id_type=MESH,
            )
            copy.start()
            copies.append(copy)
    pltpu.make_async_copy(
        row_out.at[pl.ds(0, peers - 1)], row_out.at[pl.ds(0, peers - 1)], row_send
    ).wait()
    mine = pl.ds(pl.multiple_of(hub * quarter, quarter), quarter)
    own_stat = stat_ref[hub][:, 0:quarter]
    own_self = self_ref[hub][:, 0:quarter]
    own_value = value_ref[mine, :]
    for copy in copies:
        copy.wait()

    stats = [own_stat] + [stat_in[h][:, 0:quarter] for h in range(hubs - 1)]
    agg = merge(
        [s[0:heads, :] for s in stats],
        [s[heads : 2 * heads, :] for s in stats],
        [own_value] + [value_in[h] for h in range(hubs - 1)],
        own_self,
        source_ref[mine, :],
        expand,
    )
    done_ref[...] = gru(agg, from_state_ref[mine, :], state_ref[mine, :], w_input_ref[...])
    copies = []
    for h in range(1, hubs):
        copy = pltpu.make_async_remote_copy(
            src_ref=done_ref,
            dst_ref=out_ref.at[mine, :],
            send_sem=done_send.at[h - 1],
            recv_sem=done_recv.at[h - 1],
            device_id=(me, lax.rem(hub + h, hubs)),
            device_id_type=MESH,
        )
        copy.start()
        copies.append(copy)
    out_ref[mine, :] = done_ref[...]
    for copy in copies:
        copy.wait()


def body(
    node_state,
    w_source,
    w_target,
    type_table,
    attention,
    w_input,
    w_hidden,
    edge_src,
    edge_dst,
    edge_type,
    edge_live,
):
    peers = lax.axis_size("node")
    hubs = lax.axis_size("hub")
    node_dev, width = node_state.shape
    heads = attention.shape[0]
    edges = edge_src.shape[0]
    quarter = node_dev // hubs
    inputs = (
        node_state,
        w_source,
        w_target,
        type_table,
        attention,
        w_input,
        w_hidden,
        edge_src.reshape(-1, 128),
        edge_dst.reshape(-1, 128),
        edge_type.reshape(-1, 128),
        edge_live.reshape(-1, 128),
    )
    dma = pltpu.SemaphoreType.DMA
    vmem = pltpu.VMEM
    return pl.pallas_call(
        functools.partial(kernel, peers, hubs),
        out_shape=jax.ShapeDtypeStruct((node_dev, width), bf16),
        in_specs=[pl.BlockSpec(memory_space=pl.ANY)] * 11,
        out_specs=pl.BlockSpec(memory_space=pltpu.VMEM),
        scratch_shapes=[
            vmem((peers, 1, 128), f32),
            vmem((peers, 1, 128), f32),
            vmem((peers, 2, width), bf16),
            vmem((peers, 2, width), bf16),
            vmem((node_dev, width), bf16),
            vmem((edges, node_dev), bf16),
            vmem((node_dev, edges), bf16),
            vmem((edges, 2 * peers), bf16),
            vmem((edges, width), f32),
            vmem((edges, node_dev), f32),
            vmem((edges, heads), f32),
            vmem((edges, heads), f32),
            vmem((edges, width), bf16),
            vmem((node_dev, width), bf16),
            vmem((hubs, 2 * heads, 128), f32),
            vmem((hubs - 1, quarter, width), bf16),
            vmem((hubs - 1, 2 * heads, 128), f32),
            vmem((node_dev, 3 * width), f32),
            vmem((hubs, heads, 128), f32),
            vmem((quarter, width), bf16),
            vmem((edges, width), bf16),
            vmem((edges, heads), bf16),
            dma,
            dma,
            dma,
            dma,
            dma,
            dma,
            dma((hubs - 1,)),
            dma((hubs - 1,)),
            dma((hubs - 1,)),
            dma((hubs - 1,)),
            dma((hubs - 1,)),
            dma((hubs - 1,)),
            dma((len(inputs),)),
            *[vmem(x.shape, x.dtype) for x in inputs],
        ],
        compiler_params=pltpu.CompilerParams(collective_id=0, has_side_effects=True),
        name="gat",
    )(*inputs)


def solution(mesh):
    edges = P(("node", "hub"))
    placed = (P("node", None), P(), P(), P(), P(), P(), P(), edges, edges, edges, edges)
    return jax.shard_map(
        body, mesh=mesh, in_specs=placed, out_specs=P("node", None), check_vma=False
    )
```

```python
import functools

import jax
import jax.numpy as jnp
from jax import lax
from jax.experimental import pallas as pl
from jax.experimental.pallas import tpu as pltpu
from jax.sharding import PartitionSpec as P

f32 = jnp.float32
bf16 = jnp.bfloat16
big_value = 1e30
MESH = pl.DeviceIdType.MESH
GROUP = 128


def halves(x):
    high = x.astype(bf16)
    return high, (x - high.astype(f32)).astype(bf16)


def dot(a, b):
    return jnp.dot(a, b, preferred_element_type=f32)


def dot_nt(a, b):
    return lax.dot_general(a, b, (((1,), (1,)), ((), ())), preferred_element_type=f32)


def leaky(v):
    return jnp.maximum(v, 0.2 * v)


def lane_ids(rows, lanes):
    return lax.broadcasted_iota(jnp.int32, (rows, lanes), 1).astype(f32)


def columns(flat):
    return jnp.transpose(flat.astype(f32))


def requests(src_cols, slots, node_dev):
    lanes, groups = src_cols.shape
    per = lanes // slots
    cube = src_cols.reshape(per, slots, groups)
    low = jnp.min(cube, axis=1)
    high = jnp.max(cube, axis=1)
    picked = jnp.where(cube == jnp.max(cube, axis=1, keepdims=True), 1.0, 0.0).reshape(lanes, groups)
    lane = lax.broadcasted_iota(jnp.int32, (per, 128), 1)
    row = lax.broadcasted_iota(jnp.int32, (per, 128), 0)
    out = []
    for g in range(groups):
        first = ((g * per + row) * node_dev).astype(f32)
        out.append(jnp.where(lane == 0, low[:, g : g + 1], high[:, g : g + 1]) - first)
    return out, picked


def owner_rows(asked, source):
    peers, node_dev = asked.shape[0], source.shape[0]
    ids = lane_ids(peers, node_dev)
    first = dot(jnp.where(ids == asked[:, 0:1], 1.0, 0.0).astype(bf16), source)
    second = dot(jnp.where(ids == asked[:, 1:2], 1.0, 0.0).astype(bf16), source)
    return jnp.stack([first, second], axis=1).astype(bf16)


def head_matrix(attention, width):
    heads, head_dim = attention.shape
    wide = jnp.concatenate([attention] * heads, axis=1)
    return jnp.where(head_mask(heads, width), wide, 0.0)


def head_mask(heads, width):
    head_dim = width // heads
    lane = lax.broadcasted_iota(jnp.int32, (heads, width), 1)
    row = lax.broadcasted_iota(jnp.int32, (heads, width), 0)
    return (lane >= row * head_dim) & (lane < (row + 1) * head_dim)


def scores(left, att_high, att_low):
    high, low = halves(left)
    return dot_nt(high, att_high) + (dot_nt(high, att_low) + dot_nt(low, att_high))


def scores_t(left, att_high, att_low):
    high, low = halves(left)
    return dot_nt(att_high, high) + (dot_nt(att_low, high) + dot_nt(att_high, low))


def merge(peaks, totals, values, self_t, source, expand):
    peak = self_t
    for p in peaks:
        peak = jnp.maximum(peak, p)
    scales = [jnp.exp(p - peak) for p in peaks]
    self_scale = jnp.exp(self_t - peak)
    total = self_scale
    for s, t in zip(scales, totals):
        total = total + s * t
    inverse = 1.0 / total
    coefs = jnp.concatenate([s * inverse for s in scales] + [self_scale * inverse], axis=0)
    high, low = halves(jnp.transpose(coefs))
    heads = self_t.shape[0]
    agg = None
    for d, value in enumerate(list(values) + [source]):
        part = slice(d * heads, (d + 1) * heads)
        factor = dot(high[:, part], expand) + dot(low[:, part], expand)
        term = factor * value.astype(f32)
        agg = term if agg is None else agg + term
    return agg.astype(bf16)


def gru(agg, from_state, state, w_input):
    width = state.shape[1]
    from_input = dot(agg, w_input)
    reset = jax.nn.sigmoid(from_input[:, :width] + from_state[:, :width])
    update = jax.nn.sigmoid(from_input[:, width : 2 * width] + from_state[:, width : 2 * width])
    candidate = jnp.tanh(from_input[:, 2 * width :] + reset * from_state[:, 2 * width :])
    return ((1.0 - update) * candidate + update * state.astype(f32)).astype(bf16)


def kernel(
    peers,
    hubs,
    state_any,
    w_source_any,
    w_target_any,
    type_any,
    attention_any,
    w_input_any,
    w_hidden_any,
    src_any,
    dst_any,
    kind_any,
    live_any,
    out_ref,
    ask_out,
    ask_in,
    row_out,
    row_in,
    source_ref,
    member_ref,
    member_t_ref,
    pick_ref,
    base_ref,
    mask_ref,
    dead_ref,
    score_ref,
    rows_ref,
    value_ref,
    stat_ref,
    value_in,
    stat_in,
    from_state_ref,
    self_ref,
    done_ref,
    weighted_ref,
    weight_ref,
    ask_send,
    ask_recv,
    ask_own,
    row_send,
    row_recv,
    row_own,
    value_send,
    value_recv,
    stat_send,
    stat_recv,
    done_send,
    done_recv,
    load_sem,
    state_ref,
    w_source_ref,
    w_target_ref,
    type_ref,
    attention_ref,
    w_input_ref,
    w_hidden_ref,
    src_ref,
    dst_ref,
    kind_ref,
    live_ref,
):
    me = lax.axis_index("node")
    hub = lax.axis_index("hub")
    loads = {}
    for i, (name, far, near) in enumerate(
        (
            ("state", state_any, state_ref),
            ("w_source", w_source_any, w_source_ref),
            ("w_target", w_target_any, w_target_ref),
            ("type", type_any, type_ref),
            ("attention", attention_any, attention_ref),
            ("w_input", w_input_any, w_input_ref),
            ("w_hidden", w_hidden_any, w_hidden_ref),
            ("src", src_any, src_ref),
            ("dst", dst_any, dst_ref),
            ("kind", kind_any, kind_ref),
            ("live", live_any, live_ref),
        )
    ):
        loads[name] = pltpu.make_async_copy(far, near, load_sem.at[i])
    node_dev, width = state_ref.shape
    heads = attention_ref.shape[0]
    groups = src_ref.shape[0]
    slots = groups * 128 // peers

    def each_peer(act):
        act(lax.rem(me + peers // 2, peers))

        def step(t, carry):
            act(lax.rem(me + (peers // 2 + 1 + t), peers))
            act(lax.rem(me + (peers // 2 - 1 - t), peers))
            return carry

        lax.fori_loop(0, peers // 2 - 1, step, 0)

    barrier = pltpu.get_barrier_semaphore()

    def greet(peer):
        pl.semaphore_signal(barrier, inc=1, device_id=(peer, hub), device_id_type=MESH)

    each_peer(greet)
    for h in range(1, hubs):
        pl.semaphore_signal(
            barrier, inc=1, device_id=(me, lax.rem(hub + h, hubs)), device_id_type=MESH
        )

    for name in ("src", "state", "w_source"):
        loads[name].start()
    for name in loads:
        if name not in ("src", "state", "w_source"):
            loads[name].start()
    for name in ("src", "state", "w_source"):
        loads[name].wait()
    asks, picked = requests(columns(src_ref[...]), slots, node_dev)
    per = peers // groups
    for g in range(groups):
        ask_out[g * per : (g + 1) * per, 0, :] = asks[g]
    state = state_ref[...]
    source = dot(state, w_source_ref[...]).astype(bf16)
    source_ref[...] = source

    pl.semaphore_wait(barrier, peers - 1 + hubs - 1)

    def ask(peer):
        pltpu.make_async_remote_copy(
            src_ref=ask_out.at[peer],
            dst_ref=ask_in.at[me],
            send_sem=ask_send,
            recv_sem=ask_recv,
            device_id=(peer, hub),
            device_id_type=MESH,
        ).start()

    each_peer(ask)
    own_ask = pltpu.make_async_copy(ask_out.at[me], ask_in.at[me], ask_own)
    own_ask.start()

    for name in loads:
        if name not in ("src", "state", "w_source"):
            loads[name].wait()
    target = dot(state, w_target_ref[...])
    target_high, target_low = halves(target)
    types = type_ref[...].astype(f32)
    att = head_matrix(attention_ref[...], width)
    att_high, att_low = halves(att)
    expand = jnp.where(head_mask(heads, width), 1.0, 0.0).astype(bf16)
    self_t = scores_t(
        leaky(source.astype(f32) + target + types[types.shape[0] - 1 :, :]), att_high, att_low
    )
    dst_cols = columns(dst_ref[...])
    kind_cols = columns(kind_ref[...])
    live_cols = columns(live_ref[...])
    ids = lane_ids(GROUP, node_dev)
    block = (lax.broadcasted_iota(jnp.int32, (GROUP, 1), 0) // slots).astype(f32)
    node_ids = lax.broadcasted_iota(jnp.int32, (node_dev, GROUP), 0)
    for g in range(groups):
        part = slice(g * GROUP, (g + 1) * GROUP)
        here = ids == dst_cols[:, g : g + 1]
        member = jnp.where(here, 1.0, 0.0).astype(bf16)
        member_ref[part, :] = member
        mask_ref[part, :] = jnp.where(here, 0.0, -big_value)
        member_t_ref[:, part] = jnp.where(node_ids == dst_ref[g : g + 1, :], 1.0, 0.0).astype(bf16)
        wanted = 2.0 * (g * (GROUP // slots) + block) + picked[:, g : g + 1]
        pick_ref[part, :] = jnp.where(lane_ids(GROUP, 2 * peers) == wanted, 1.0, 0.0).astype(bf16)
        kind = kind_cols[:, g : g + 1]
        kinds = types[0:1, :]
        for t in range(1, types.shape[0]):
            kinds = jnp.where(kind == float(t), types[t : t + 1, :], kinds)
        base_ref[part, :] = dot(member, target_high) + dot(member, target_low) + kinds
        dead_ref[part, :] = jnp.broadcast_to(
            jnp.where(live_cols[:, g : g + 1] > 0.0, 0.0, -big_value), (GROUP, heads)
        )

    own_ask.wait()
    pltpu.make_async_copy(
        ask_in.at[pl.ds(0, peers - 1)], ask_in.at[pl.ds(0, peers - 1)], ask_recv
    ).wait()
    row_out[...] = owner_rows(ask_in[:, 0, :], source_ref[...])

    def reply(peer):
        pltpu.make_async_remote_copy(
            src_ref=row_out.at[peer],
            dst_ref=row_in.at[me],
            send_sem=row_send,
            recv_sem=row_recv,
            device_id=(peer, hub),
            device_id_type=MESH,
        ).start()

    each_peer(reply)
    own_row = pltpu.make_async_copy(row_out.at[me], row_in.at[me], row_own)
    own_row.start()
    from_state_ref[...] = dot(state_ref[...], w_hidden_ref[...])
    pltpu.make_async_copy(
        ask_out.at[pl.ds(0, peers - 1)], ask_out.at[pl.ds(0, peers - 1)], ask_send
    ).wait()
    own_row.wait()
    pltpu.make_async_copy(
        row_in.at[pl.ds(0, peers - 1)], row_in.at[pl.ds(0, peers - 1)], row_recv
    ).wait()

    fetched = row_in[...].reshape(2 * peers, width)

    peak = self_t
    for g in range(groups):
        part = slice(g * GROUP, (g + 1) * GROUP)
        rows = dot(pick_ref[part, :], fetched)
        rows_ref[part, :] = rows.astype(bf16)
        score = scores(leaky(rows + base_ref[part, :]), att_high, att_low) + dead_ref[part, :]
        score_ref[part, :] = score
        mask = mask_ref[part, :]
        fresh = [jnp.max(score[:, h : h + 1] + mask, axis=0, keepdims=True) for h in range(heads)]
        peak = jnp.maximum(peak, jnp.concatenate(fresh, axis=0))
    peak_high, peak_low = halves(peak)
    peak = peak_high.astype(f32) + peak_low.astype(f32)

    for g in range(groups):
        part = slice(g * GROUP, (g + 1) * GROUP)
        member = member_ref[part, :]
        edge_peak = dot_nt(member, peak_high) + dot_nt(member, peak_low)
        weight = jnp.exp(score_ref[part, :] - edge_peak).astype(bf16)
        weight_ref[part, :] = weight
        rows = rows_ref[part, :].astype(f32)
        weighted_ref[part, :] = (dot(weight, expand) * rows).astype(bf16)
    total = dot(member_t_ref[...], weight_ref[...])
    value = dot(member_t_ref[...], weighted_ref[...])
    value_ref[...] = value.astype(bf16)
    quarter = node_dev // hubs
    total_t = jnp.transpose(total)
    for h in range(hubs):
        nodes = slice(h * quarter, (h + 1) * quarter)
        stat_ref[h] = jnp.concatenate([peak[:, nodes], total_t[:, nodes]], axis=1)
        self_ref[h, :, 0:quarter] = self_t[:, nodes]

    order = sorted(range(1, hubs), key=lambda h: abs(h - hubs / 2))
    copies = []
    for h in order:
        other = lax.rem(hub + h, hubs)
        theirs = pl.ds(pl.multiple_of(other * quarter, quarter), quarter)
        for source_buf, target_buf, send, recv in (
            (stat_ref.at[other], stat_in, stat_send, stat_recv),
            (value_ref.at[theirs, :], value_in, value_send, value_recv),
        ):
            copy = pltpu.make_async_remote_copy(
                src_ref=source_buf,
                dst_ref=target_buf.at[h - 1],
                send_sem=send.at[h - 1],
                recv_sem=recv.at[h - 1],
                device_id=(me, other),
                device_id_type=MESH,
            )
            copy.start()
            copies.append(copy)
    pltpu.make_async_copy(
        row_out.at[pl.ds(0, peers - 1)], row_out.at[pl.ds(0, peers - 1)], row_send
    ).wait()
    mine = pl.ds(pl.multiple_of(hub * quarter, quarter), quarter)
    own_stat = stat_ref[hub]
    own_self = self_ref[hub][:, 0:quarter]
    own_value = value_ref[mine, :]
    for copy in copies:
        copy.wait()

    stats = [own_stat] + [stat_in[h] for h in range(hubs - 1)]
    agg = merge(
        [s[:, 0:quarter] for s in stats],
        [s[:, quarter:] for s in stats],
        [own_value] + [value_in[h] for h in range(hubs - 1)],
        own_self,
        source_ref[mine, :],
        expand,
    )
    done_ref[...] = gru(agg, from_state_ref[mine, :], state_ref[mine, :], w_input_ref[...])
    copies = []
    for h in order:
        copy = pltpu.make_async_remote_copy(
            src_ref=done_ref,
            dst_ref=out_ref.at[mine, :],
            send_sem=done_send.at[h - 1],
            recv_sem=done_recv.at[h - 1],
            device_id=(me, lax.rem(hub + h, hubs)),
            device_id_type=MESH,
        )
        copy.start()
        copies.append(copy)
    out_ref[mine, :] = done_ref[...]
    for copy in copies:
        copy.wait()


def body(
    node_state,
    w_source,
    w_target,
    type_table,
    attention,
    w_input,
    w_hidden,
    edge_src,
    edge_dst,
    edge_type,
    edge_live,
):
    peers = lax.axis_size("node")
    hubs = lax.axis_size("hub")
    node_dev, width = node_state.shape
    heads = attention.shape[0]
    edges = edge_src.shape[0]
    quarter = node_dev // hubs
    inputs = (
        node_state,
        w_source,
        w_target,
        type_table,
        attention,
        w_input,
        w_hidden,
        edge_src.reshape(-1, 128),
        edge_dst.reshape(-1, 128),
        edge_type.reshape(-1, 128),
        edge_live.reshape(-1, 128),
    )
    dma = pltpu.SemaphoreType.DMA
    vmem = pltpu.VMEM
    return pl.pallas_call(
        functools.partial(kernel, peers, hubs),
        out_shape=jax.ShapeDtypeStruct((node_dev, width), bf16),
        in_specs=[pl.BlockSpec(memory_space=pl.ANY)] * 11,
        out_specs=pl.BlockSpec(memory_space=pltpu.VMEM),
        scratch_shapes=[
            vmem((peers, 1, 128), f32),
            vmem((peers, 1, 128), f32),
            vmem((peers, 2, width), bf16),
            vmem((peers, 2, width), bf16),
            vmem((node_dev, width), bf16),
            vmem((edges, node_dev), bf16),
            vmem((node_dev, edges), bf16),
            vmem((edges, 2 * peers), bf16),
            vmem((edges, width), f32),
            vmem((edges, node_dev), f32),
            vmem((edges, heads), f32),
            vmem((edges, heads), f32),
            vmem((edges, width), bf16),
            vmem((node_dev, width), bf16),
            vmem((hubs, heads, 2 * quarter), f32),
            vmem((hubs - 1, quarter, width), bf16),
            vmem((hubs - 1, heads, 2 * quarter), f32),
            vmem((node_dev, 3 * width), f32),
            vmem((hubs, heads, 128), f32),
            vmem((quarter, width), bf16),
            vmem((edges, width), bf16),
            vmem((edges, heads), bf16),
            dma,
            dma,
            dma,
            dma,
            dma,
            dma,
            dma((hubs - 1,)),
            dma((hubs - 1,)),
            dma((hubs - 1,)),
            dma((hubs - 1,)),
            dma((hubs - 1,)),
            dma((hubs - 1,)),
            dma((len(inputs),)),
            *[vmem(x.shape, x.dtype) for x in inputs],
        ],
        compiler_params=pltpu.CompilerParams(collective_id=0, has_side_effects=True),
        name="gat",
    )(*inputs)


def solution(mesh):
    edges = P(("node", "hub"))
    placed = (P("node", None), P(), P(), P(), P(), P(), P(), edges, edges, edges, edges)
    return jax.shard_map(
        body, mesh=mesh, in_specs=placed, out_specs=P("node", None), check_vma=False
    )
```

```python
import functools

import jax
import jax.numpy as jnp
from jax import lax
from jax.experimental import pallas as pl
from jax.experimental.pallas import tpu as pltpu
from jax.sharding import PartitionSpec as P

f32 = jnp.float32
bf16 = jnp.bfloat16
big_value = 1e30
MESH = pl.DeviceIdType.MESH
GROUP = 128


def halves(x):
    high = x.astype(bf16)
    return high, (x - high.astype(f32)).astype(bf16)


def dot(a, b):
    return jnp.dot(a, b, preferred_element_type=f32)


def dot_nt(a, b):
    return lax.dot_general(a, b, (((1,), (1,)), ((), ())), preferred_element_type=f32)


def leaky(v):
    return jnp.maximum(v, 0.2 * v)


def lane_ids(rows, lanes):
    return lax.broadcasted_iota(jnp.int32, (rows, lanes), 1).astype(f32)


def columns(flat):
    return jnp.transpose(flat.astype(f32))


def requests(src_cols, slots, node_dev):
    lanes, groups = src_cols.shape
    per = lanes // slots
    cube = src_cols.reshape(per, slots, groups)
    low = jnp.min(cube, axis=1)
    high = jnp.max(cube, axis=1)
    picked = jnp.where(cube == jnp.max(cube, axis=1, keepdims=True), 1.0, 0.0).reshape(lanes, groups)
    lane = lax.broadcasted_iota(jnp.int32, (per, 128), 1)
    row = lax.broadcasted_iota(jnp.int32, (per, 128), 0)
    out = []
    for g in range(groups):
        first = ((g * per + row) * node_dev).astype(f32)
        out.append(jnp.where(lane == 0, low[:, g : g + 1], high[:, g : g + 1]) - first)
    return out, picked


def owner_rows(asked, source):
    peers, node_dev = asked.shape[0], source.shape[0]
    ids = lane_ids(peers, node_dev)
    first = dot(jnp.where(ids == asked[:, 0:1], 1.0, 0.0).astype(bf16), source)
    second = dot(jnp.where(ids == asked[:, 1:2], 1.0, 0.0).astype(bf16), source)
    return jnp.stack([first, second], axis=1).astype(bf16)


def head_matrix(attention, width):
    heads, head_dim = attention.shape
    wide = jnp.concatenate([attention] * heads, axis=1)
    return jnp.where(head_mask(heads, width), wide, 0.0)


def head_mask(heads, width):
    head_dim = width // heads
    lane = lax.broadcasted_iota(jnp.int32, (heads, width), 1)
    row = lax.broadcasted_iota(jnp.int32, (heads, width), 0)
    return (lane >= row * head_dim) & (lane < (row + 1) * head_dim)


def scores(left, att_high, att_low):
    high, low = halves(left)
    return dot_nt(high, att_high) + (dot_nt(high, att_low) + dot_nt(low, att_high))


def scores_t(left, att_high, att_low):
    high, low = halves(left)
    return dot_nt(att_high, high) + (dot_nt(att_low, high) + dot_nt(att_high, low))


def merge(peaks, totals, values, self_t, source, expand):
    peak = self_t
    for p in peaks:
        peak = jnp.maximum(peak, p)
    scales = [jnp.exp(p - peak) for p in peaks]
    self_scale = jnp.exp(self_t - peak)
    total = self_scale
    for s, t in zip(scales, totals):
        total = total + s * t
    inverse = 1.0 / total
    coefs = jnp.concatenate([s * inverse for s in scales] + [self_scale * inverse], axis=0)
    high, low = halves(jnp.transpose(coefs))
    heads = self_t.shape[0]
    agg = None
    for d, value in enumerate(list(values) + [source]):
        part = slice(d * heads, (d + 1) * heads)
        factor = dot(high[:, part], expand) + dot(low[:, part], expand)
        term = factor * value.astype(f32)
        agg = term if agg is None else agg + term
    return agg.astype(bf16)


def gru(agg, from_state, state, w_input):
    width = state.shape[1]
    from_input = dot(agg, w_input)
    reset = jax.nn.sigmoid(from_input[:, :width] + from_state[:, :width])
    update = jax.nn.sigmoid(from_input[:, width : 2 * width] + from_state[:, width : 2 * width])
    candidate = jnp.tanh(from_input[:, 2 * width :] + reset * from_state[:, 2 * width :])
    return ((1.0 - update) * candidate + update * state.astype(f32)).astype(bf16)


def kernel(
    peers,
    hubs,
    state_any,
    w_source_any,
    w_target_any,
    type_any,
    attention_any,
    w_input_any,
    w_hidden_any,
    src_any,
    dst_any,
    kind_any,
    live_any,
    out_ref,
    ask_out,
    ask_in,
    row_out,
    row_in,
    source_ref,
    member_ref,
    member_t_ref,
    pick_ref,
    base_ref,
    mask_ref,
    dead_ref,
    score_ref,
    rows_ref,
    value_ref,
    stat_ref,
    value_in,
    stat_in,
    from_state_ref,
    self_ref,
    done_ref,
    weighted_ref,
    weight_ref,
    ask_send,
    ask_recv,
    ask_own,
    row_send,
    row_recv,
    row_own,
    value_send,
    value_recv,
    stat_send,
    stat_recv,
    done_send,
    done_recv,
    load_sem,
    state_ref,
    w_source_ref,
    w_target_ref,
    type_ref,
    attention_ref,
    w_input_ref,
    w_hidden_ref,
    src_ref,
    dst_ref,
    kind_ref,
    live_ref,
):
    me = lax.axis_index("node")
    hub = lax.axis_index("hub")
    loads = {}
    for i, (name, far, near) in enumerate(
        (
            ("state", state_any, state_ref),
            ("w_source", w_source_any, w_source_ref),
            ("w_target", w_target_any, w_target_ref),
            ("type", type_any, type_ref),
            ("attention", attention_any, attention_ref),
            ("w_input", w_input_any, w_input_ref),
            ("w_hidden", w_hidden_any, w_hidden_ref),
            ("src", src_any, src_ref),
            ("dst", dst_any, dst_ref),
            ("kind", kind_any, kind_ref),
            ("live", live_any, live_ref),
        )
    ):
        loads[name] = pltpu.make_async_copy(far, near, load_sem.at[i])
    node_dev, width = state_ref.shape
    heads = attention_ref.shape[0]
    groups = src_ref.shape[0]
    slots = groups * 128 // peers

    def each_peer(act):
        act(lax.rem(me + peers // 2, peers))

        def step(t, carry):
            act(lax.rem(me + (peers // 2 + 1 + t), peers))
            act(lax.rem(me + (peers // 2 - 1 - t), peers))
            return carry

        lax.fori_loop(0, peers // 2 - 1, step, 0)

    barrier = pltpu.get_barrier_semaphore()

    def greet(peer):
        pl.semaphore_signal(barrier, inc=1, device_id=(peer, hub), device_id_type=MESH)

    each_peer(greet)
    for h in range(1, hubs):
        pl.semaphore_signal(
            barrier, inc=1, device_id=(me, lax.rem(hub + h, hubs)), device_id_type=MESH
        )

    for name in ("src", "state", "w_source"):
        loads[name].start()
    for name in loads:
        if name not in ("src", "state", "w_source"):
            loads[name].start()
    for name in ("src", "state", "w_source"):
        loads[name].wait()
    asks, picked = requests(columns(src_ref[...]), slots, node_dev)
    per = peers // groups
    for g in range(groups):
        ask_out[g * per : (g + 1) * per, 0, :] = asks[g]
    state = state_ref[...]
    source = dot(state, w_source_ref[...]).astype(bf16)
    source_ref[...] = source

    pl.semaphore_wait(barrier, peers - 1 + hubs - 1)

    def ask(peer):
        pltpu.make_async_remote_copy(
            src_ref=ask_out.at[peer],
            dst_ref=ask_in.at[me],
            send_sem=ask_send,
            recv_sem=ask_recv,
            device_id=(peer, hub),
            device_id_type=MESH,
        ).start()

    each_peer(ask)
    own_ask = pltpu.make_async_copy(ask_out.at[me], ask_in.at[me], ask_own)
    own_ask.start()

    for name in loads:
        if name not in ("src", "state", "w_source"):
            loads[name].wait()
    target = dot(state, w_target_ref[...])
    target_high, target_low = halves(target)
    types = type_ref[...].astype(f32)
    att = head_matrix(attention_ref[...], width)
    att_high, att_low = halves(att)
    expand = jnp.where(head_mask(heads, width), 1.0, 0.0).astype(bf16)
    self_t = scores_t(
        leaky(source.astype(f32) + target + types[types.shape[0] - 1 :, :]), att_high, att_low
    )
    dst_cols = columns(dst_ref[...])
    kind_cols = columns(kind_ref[...])
    live_cols = columns(live_ref[...])
    ids = lane_ids(GROUP, node_dev)
    block = (lax.broadcasted_iota(jnp.int32, (GROUP, 1), 0) // slots).astype(f32)
    node_ids = lax.broadcasted_iota(jnp.int32, (node_dev, GROUP), 0)
    for g in range(groups):
        part = slice(g * GROUP, (g + 1) * GROUP)
        here = ids == dst_cols[:, g : g + 1]
        member = jnp.where(here, 1.0, 0.0).astype(bf16)
        member_ref[part, :] = member
        mask_ref[part, :] = jnp.where(here, 0.0, -big_value)
        member_t_ref[:, part] = jnp.where(node_ids == dst_ref[g : g + 1, :], 1.0, 0.0).astype(bf16)
        wanted = 2.0 * (g * (GROUP // slots) + block) + picked[:, g : g + 1]
        pick_ref[part, :] = jnp.where(lane_ids(GROUP, 2 * peers) == wanted, 1.0, 0.0).astype(bf16)
        kind = kind_cols[:, g : g + 1]
        kinds = types[0:1, :]
        for t in range(1, types.shape[0]):
            kinds = jnp.where(kind == float(t), types[t : t + 1, :], kinds)
        base_ref[part, :] = dot(member, target_high) + dot(member, target_low) + kinds
        dead_ref[part, :] = jnp.broadcast_to(
            jnp.where(live_cols[:, g : g + 1] > 0.0, 0.0, -big_value), (GROUP, heads)
        )

    own_ask.wait()
    pltpu.make_async_copy(
        ask_in.at[pl.ds(0, peers - 1)], ask_in.at[pl.ds(0, peers - 1)], ask_recv
    ).wait()
    row_out[...] = owner_rows(ask_in[:, 0, :], source_ref[...])

    def reply(peer):
        pltpu.make_async_remote_copy(
            src_ref=row_out.at[peer],
            dst_ref=row_in.at[me],
            send_sem=row_send,
            recv_sem=row_recv,
            device_id=(peer, hub),
            device_id_type=MESH,
        ).start()

    each_peer(reply)
    own_row = pltpu.make_async_copy(row_out.at[me], row_in.at[me], row_own)
    own_row.start()
    from_state_ref[...] = dot(state_ref[...], w_hidden_ref[...])
    pltpu.make_async_copy(
        ask_out.at[pl.ds(0, peers - 1)], ask_out.at[pl.ds(0, peers - 1)], ask_send
    ).wait()
    own_row.wait()
    pltpu.make_async_copy(
        row_in.at[pl.ds(0, peers - 1)], row_in.at[pl.ds(0, peers - 1)], row_recv
    ).wait()

    fetched = row_in[...].reshape(2 * peers, width)

    peak = self_t
    for g in range(groups):
        part = slice(g * GROUP, (g + 1) * GROUP)
        rows = dot(pick_ref[part, :], fetched)
        rows_ref[part, :] = rows.astype(bf16)
        score = scores(leaky(rows + base_ref[part, :]), att_high, att_low) + dead_ref[part, :]
        score_ref[part, :] = score
        mask = mask_ref[part, :]
        fresh = [jnp.max(score[:, h : h + 1] + mask, axis=0, keepdims=True) for h in range(heads)]
        peak = jnp.maximum(peak, jnp.concatenate(fresh, axis=0))
    peak_high, peak_low = halves(peak)
    peak = peak_high.astype(f32) + peak_low.astype(f32)

    for g in range(groups):
        part = slice(g * GROUP, (g + 1) * GROUP)
        member = member_ref[part, :]
        edge_peak = dot_nt(member, peak_high) + dot_nt(member, peak_low)
        weight = jnp.exp(score_ref[part, :] - edge_peak).astype(bf16)
        weight_ref[part, :] = weight
        rows = rows_ref[part, :].astype(f32)
        weighted_ref[part, :] = (dot(weight, expand) * rows).astype(bf16)
    total = dot(member_t_ref[...], weight_ref[...])
    quarter = node_dev // hubs
    total_t = jnp.transpose(total)
    for h in range(hubs):
        nodes = slice(h * quarter, (h + 1) * quarter)
        stat_ref[h] = jnp.concatenate([peak[:, nodes], total_t[:, nodes]], axis=1)
        self_ref[h, :, 0:quarter] = self_t[:, nodes]

    order = sorted(range(1, hubs), key=lambda h: abs(h - hubs / 2))
    copies = []

    def to_hub(h, source_buf, target_buf, send, recv):
        copy = pltpu.make_async_remote_copy(
            src_ref=source_buf,
            dst_ref=target_buf,
            send_sem=send,
            recv_sem=recv,
            device_id=(me, lax.rem(hub + h, hubs)),
            device_id_type=MESH,
        )
        copy.start()
        copies.append(copy)

    for h in order:
        i = h - 1
        theirs = stat_ref.at[lax.rem(hub + h, hubs)]
        to_hub(h, theirs, stat_in.at[i], stat_send.at[i], stat_recv.at[i])
    for c in range(2):
        cols = slice(c * width // 2, (c + 1) * width // 2)
        value_ref[:, cols] = dot(member_t_ref[...], weighted_ref[:, cols]).astype(bf16)
        for h in order:
            i = h - 1
            start = lax.rem(hub + h, hubs) * quarter
            theirs = value_ref.at[pl.ds(pl.multiple_of(start, quarter), quarter), cols]
            to_hub(h, theirs, value_in.at[i, :, cols], value_send.at[c, i], value_recv.at[c, i])
    pltpu.make_async_copy(
        row_out.at[pl.ds(0, peers - 1)], row_out.at[pl.ds(0, peers - 1)], row_send
    ).wait()
    mine = pl.ds(pl.multiple_of(hub * quarter, quarter), quarter)
    own_stat = stat_ref[hub]
    own_self = self_ref[hub][:, 0:quarter]
    own_value = value_ref[mine, :]
    for copy in copies:
        copy.wait()

    stats = [own_stat] + [stat_in[h] for h in range(hubs - 1)]
    agg = merge(
        [s[:, 0:quarter] for s in stats],
        [s[:, quarter:] for s in stats],
        [own_value] + [value_in[h] for h in range(hubs - 1)],
        own_self,
        source_ref[mine, :],
        expand,
    )
    done_ref[...] = gru(agg, from_state_ref[mine, :], state_ref[mine, :], w_input_ref[...])
    copies = []
    for h in order:
        copy = pltpu.make_async_remote_copy(
            src_ref=done_ref,
            dst_ref=out_ref.at[mine, :],
            send_sem=done_send.at[h - 1],
            recv_sem=done_recv.at[h - 1],
            device_id=(me, lax.rem(hub + h, hubs)),
            device_id_type=MESH,
        )
        copy.start()
        copies.append(copy)
    out_ref[mine, :] = done_ref[...]
    for copy in copies:
        copy.wait()


def body(
    node_state,
    w_source,
    w_target,
    type_table,
    attention,
    w_input,
    w_hidden,
    edge_src,
    edge_dst,
    edge_type,
    edge_live,
):
    peers = lax.axis_size("node")
    hubs = lax.axis_size("hub")
    node_dev, width = node_state.shape
    heads = attention.shape[0]
    edges = edge_src.shape[0]
    quarter = node_dev // hubs
    inputs = (
        node_state,
        w_source,
        w_target,
        type_table,
        attention,
        w_input,
        w_hidden,
        edge_src.reshape(-1, 128),
        edge_dst.reshape(-1, 128),
        edge_type.reshape(-1, 128),
        edge_live.reshape(-1, 128),
    )
    dma = pltpu.SemaphoreType.DMA
    vmem = pltpu.VMEM
    return pl.pallas_call(
        functools.partial(kernel, peers, hubs),
        out_shape=jax.ShapeDtypeStruct((node_dev, width), bf16),
        in_specs=[pl.BlockSpec(memory_space=pl.ANY)] * 11,
        out_specs=pl.BlockSpec(memory_space=pltpu.VMEM),
        scratch_shapes=[
            vmem((peers, 1, 128), f32),
            vmem((peers, 1, 128), f32),
            vmem((peers, 2, width), bf16),
            vmem((peers, 2, width), bf16),
            vmem((node_dev, width), bf16),
            vmem((edges, node_dev), bf16),
            vmem((node_dev, edges), bf16),
            vmem((edges, 2 * peers), bf16),
            vmem((edges, width), f32),
            vmem((edges, node_dev), f32),
            vmem((edges, heads), f32),
            vmem((edges, heads), f32),
            vmem((edges, width), bf16),
            vmem((node_dev, width), bf16),
            vmem((hubs, heads, 2 * quarter), f32),
            vmem((hubs - 1, quarter, width), bf16),
            vmem((hubs - 1, heads, 2 * quarter), f32),
            vmem((node_dev, 3 * width), f32),
            vmem((hubs, heads, 128), f32),
            vmem((quarter, width), bf16),
            vmem((edges, width), bf16),
            vmem((edges, heads), bf16),
            dma,
            dma,
            dma,
            dma,
            dma,
            dma,
            dma((2, hubs - 1)),
            dma((2, hubs - 1)),
            dma((hubs - 1,)),
            dma((hubs - 1,)),
            dma((hubs - 1,)),
            dma((hubs - 1,)),
            dma((len(inputs),)),
            *[vmem(x.shape, x.dtype) for x in inputs],
        ],
        compiler_params=pltpu.CompilerParams(collective_id=0, has_side_effects=True),
        name="gat",
    )(*inputs)


def solution(mesh):
    edges = P(("node", "hub"))
    placed = (P("node", None), P(), P(), P(), P(), P(), P(), edges, edges, edges, edges)
    return jax.shard_map(
        body, mesh=mesh, in_specs=placed, out_specs=P("node", None), check_vma=False
    )
```
